32 devices in a mesh: groups: 2 (over y), blk: 4 (over x, core), req: 4 (over z).
Axes of the slice: x: 2, y: 2, z: 4, core: 2. Of those that a mesh axis runs over, the one named last changes fastest.
Arguments:
- hidden_states: bfloat16 [640, 4608], P(('groups', 'req'), 'blk'), parts along dimension 0, may hold values from -12 to 12
- context_lengths: int32 [128], P(('groups', 'req')), parts along dimension 0, may hold values from 64 to 512
- cache_keys: bfloat16 [128, 512, 16, 128], P(('groups', 'req'), None, 'blk'), parts along dimension 0, may hold values from -1400 to 1400
- cache_values: bfloat16 [128, 512, 16, 128], P(('groups', 'req'), None, 'blk'), parts along dimension 0, may hold values from -6 to 6
- q_weight: bfloat16 [4608, 4096], P('req', 'blk'), may hold values from -0.09375 to 0.09375
- k_weight: bfloat16 [4608, 2048], P('req', 'blk'), may hold values from -0.09375 to 0.09375
- v_weight: bfloat16 [4608, 2048], P('req', 'blk'), may hold values from -0.09375 to 0.09375
- o_weight: bfloat16 [4096, 4608], P('blk'), may hold values from -1 to 1
- gate_weight: bfloat16 [18432, 4608], P(('blk', 'req')), may hold values from -0.09375 to 0.09375
- up_weight: bfloat16 [18432, 4608], P(('blk', 'req')), may hold values from -0.09375 to 0.09375
- down_weight: bfloat16 [18432, 4608], P(('blk', 'req')), may hold values from -0.0625 to 0.0625
- attn_gain: float32 [4608], P('blk'), may hold values from 0.1 to 1.9
- post_attn_gain: float32 [4608], P('blk'), may hold values from 0.1 to 1.9
- ffn_gain: float32 [4608], P('blk'), may hold values from 0.1 to 1.9
- post_ffn_gain: float32 [4608], P('blk'), may hold values from 0.1 to 1.9
Outputs:
- layer_output: bfloat16 [640, 4608], P(('groups', 'req'), 'blk'), parts along dimension 0
- draft_keys: bfloat16 [128, 5, 16, 128], P(('groups', 'req'), None, 'blk'), parts along dimension 0
- draft_values: bfloat16 [128, 5, 16, 128], P(('groups', 'req'), None, 'blk'), parts along dimension 0
The draws below stay inside these ranges and needn't reach their ends.
There are 2 independent parts, one for each index of `groups`. The reference program is written for one: setup_inputs(seed, part) draws one part's arguments, and reference() takes and returns one part's arrays. A program takes and returns all parts, laid end to end along the dimension named above; an argument that names none is the same for every part. Nothing has to cross between parts.
All inputs are finite; a program needn't handle non-finite values.
Results may differ from the reference program's by a relative error of at most 0.015.
Values may be sent and summed in bfloat16 or wider, within the bound.
A program may use at most 128 MiB of HBM per device.

```python
import math
import jax
import jax.numpy as jnp
from jax import lax

D = 4608
HEADS = 32
KV_HEADS = 16
HEAD_DIM = 128
FF = 18432
CTX = 512
DRAFT = 5
REQUESTS = 64
TOKENS = 320


def draw_hidden_states(key, part):
    keys = jax.random.split(jax.random.fold_in(key, 11), 3)
    columns = jnp.arange(D, dtype=jnp.float32) / max(D - 1, 1)
    entries = jax.random.normal(keys[0], (TOKENS, D), jnp.float32)
    row_scale = jnp.exp(jax.random.uniform(keys[1], (TOKENS, 1), jnp.float32, math.log(0.3), math.log(3.0)))
    column_scale = jnp.exp(math.log(3.0) * columns)[None, :] * jnp.exp(jax.random.uniform(keys[2], (1, D), jnp.float32, 0.0, math.log(2.0))) * 0.6
    values = entries * row_scale * column_scale
    return jnp.clip(values, -12.0, 12.0).astype(jnp.bfloat16)


def draw_cache_keys(key, part):
    keys = jax.random.split(jax.random.fold_in(key, 23), 1)
    shape = (REQUESTS, CTX, KV_HEADS, HEAD_DIM)
    values = jnp.clip(jax.random.normal(keys[0], shape, jnp.float32), -6.0, 6.0)
    return values.astype(jnp.bfloat16)


def draw_o_weight(key, part):
    keys = jax.random.split(jax.random.fold_in(key, 37), 2)
    fan_rows = HEADS * HEAD_DIM
    columns = jnp.arange(D, dtype=jnp.float32) / max(D - 1, 1)
    rough = jnp.exp(jax.random.uniform(keys[1], (1, D), jnp.float32, 0.0, math.log(2.0)))
    entries = jnp.clip(jax.random.normal(keys[0], (fan_rows, D), jnp.float32), -6.0, 6.0)
    column_scale = jnp.exp(math.log(4.0) * columns)[None, :] * rough * 0.4
    values = entries * column_scale * fan_rows ** (-0.5)
    return jnp.clip(values, -1.0, 1.0).astype(jnp.bfloat16)


def set_ends(array, stream_key, smallest, largest):
    extent = array.shape
    spot = [jax.random.randint(jax.random.fold_in(stream_key, axis), (), 0, extent[axis]) for axis in range(len(extent))]
    array = array.at[tuple(spot)].set(smallest)
    longest = extent.index(max(extent))
    spot[longest] = (spot[longest] + 1) % extent[longest]
    return array.at[tuple(spot)].set(largest)


def with_spikes(values, stream_key, source, target, blocks, factor):
    def block_of(dim):
        return (jnp.arange(values.shape[dim]) // (values.shape[dim] // blocks)).reshape((-1,) + (1,) * (values.ndim - 1 - dim))

    first = jax.random.permutation(stream_key, blocks)[block_of(target)]
    second = (block_of(target) + blocks // 2) % blocks
    return jnp.where((block_of(source) == first) | (block_of(source) == second), factor * values, values)


def level_of(own_key, extent, cuts, smallest, largest):
    level, own = 1.0, jax.random.fold_in(own_key, 6)
    for axis_at, blocks in cuts:
        heights = jnp.exp(jax.random.uniform(jax.random.fold_in(own, axis_at), (blocks,), jnp.float32, smallest / len(cuts), largest / len(cuts)))
        level = level * jnp.repeat(heights, extent[axis_at] // blocks).reshape([-1 if axis == axis_at else 1 for axis in range(len(extent))])
    return level


def scatter_about(own_key, extent, scale, bound, cuts=(), kind=jnp.bfloat16):
    values = jax.random.normal(own_key, extent, jnp.float32) * scale
    if len(cuts) > 0:
        values = level_of(own_key, extent, cuts, -0.22, 0.18) * values
    return jnp.clip(values, min=-bound, max=bound).astype(kind)


def gaussian_with(rng, extent, spread, bound, pieces, heavy, kind=jnp.bfloat16):
    values = spread * jax.random.normal(rng, extent, jnp.float32)
    if pieces:
        values = values * level_of(rng, extent, pieces, -0.22, 0.18)
    return jnp.clip(with_spikes(values, jax.random.fold_in(rng, 3), *heavy), -bound, bound).astype(kind)


def setup_inputs(seed: int = 0, part: int = 0) -> dict:
    key_list = jax.random.split(jax.random.key(seed), 16)
    part_splits = jax.random.split(jax.random.fold_in(key_list[15], part), 16)
    hidden_states = draw_hidden_states(jax.random.fold_in(jax.random.fold_in(key_list[15], part), 71), part)
    context_lengths = set_ends(jax.random.randint(part_splits[1], (REQUESTS,), CTX // 8, CTX + 1), jax.random.fold_in(part_splits[1], 1), CTX // 8, CTX).astype(jnp.int32)
    cache_keys = draw_cache_keys(jax.random.fold_in(jax.random.fold_in(key_list[15], part), 71), part)
    cache_values = scatter_about(part_splits[3], (REQUESTS, CTX, KV_HEADS, HEAD_DIM), 1.0, 6.0, ((0, 4), (2, 4)))
    q_weight = scatter_about(key_list[4], (D, HEADS * HEAD_DIM), D ** -0.5, 0.09375, ((0, 4), (1, 4)))
    k_weight = scatter_about(key_list[5], (D, KV_HEADS * HEAD_DIM), D ** -0.5, 0.09375, ((0, 4), (1, 4)))
    v_weight = scatter_about(key_list[6], (D, KV_HEADS * HEAD_DIM), D ** -0.5, 0.09375, ((0, 4), (1, 4)))
    o_weight = draw_o_weight(jax.random.fold_in(key_list[15], 71), part)
    gate_weight = scatter_about(key_list[8], (FF, D), D ** -0.5, 0.09375, ((0, 16),))
    up_weight = scatter_about(key_list[9], (FF, D), D ** -0.5, 0.09375, ((0, 16),))
    down_weight = gaussian_with(key_list[10], (FF, D), FF ** -0.5, 0.0625, ((0, 16),), (0, 1, 16, 2.0))
    attn_gain = jnp.clip(1.0 + 0.18 * jax.random.normal(key_list[11], (D,), jnp.float32), 0.1, 1.9)
    post_attn_gain = jnp.clip(1.0 + 0.18 * jax.random.normal(key_list[12], (D,), jnp.float32), 0.1, 1.9)
    ffn_gain = jnp.clip(1.0 + 0.18 * jax.random.normal(key_list[13], (D,), jnp.float32), 0.1, 1.9)
    post_ffn_gain = jnp.clip(1.0 + 0.18 * jax.random.normal(key_list[14], (D,), jnp.float32), 0.1, 1.9)
    return dict(hidden_states=hidden_states, context_lengths=context_lengths, cache_keys=cache_keys, cache_values=cache_values, q_weight=q_weight, k_weight=k_weight, v_weight=v_weight, o_weight=o_weight, gate_weight=gate_weight, up_weight=up_weight, down_weight=down_weight, attn_gain=attn_gain, post_attn_gain=post_attn_gain, ffn_gain=ffn_gain, post_ffn_gain=post_ffn_gain)


EPSILON = 1e-06
NEGATIVE = -1e+30

def rotate(values, positions):
    size = values.shape[-1]
    half = size // 2
    rates = 10000.0 ** (-(jnp.arange(half, dtype=jnp.float32) * 2.0) / size)
    angle = positions.astype(jnp.float32)[..., None] * rates
    cosine = jnp.cos(angle)
    sine = jnp.sin(angle)
    first = values[..., :half]
    second = values[..., half:]
    return jnp.concatenate([first * cosine - second * sine, second * cosine + first * sine], axis=-1)

def scaling(total):
    return lax.rsqrt(total / D + EPSILON)[:, None]

def attend_one(operands):
    queries, new_keys, new_values, old_keys, old_values, length = operands
    steps, heads, size = queries.shape
    shared = new_keys.shape[1]
    group = heads // shared
    scale = (D // HEADS) ** (-0.5)
    grouped = queries.reshape(steps, shared, group, size).astype(jnp.float32)
    older = jnp.einsum('skge,cke->kgsc', grouped, old_keys.astype(jnp.float32)) * scale
    newer = jnp.einsum('skge,tke->kgst', grouped, new_keys.astype(jnp.float32)) * scale
    valid = jnp.arange(old_keys.shape[0], dtype=jnp.int32) < length
    older = jnp.where(valid, older, NEGATIVE)
    causal = jnp.arange(steps, dtype=jnp.int32)[:, None] >= jnp.arange(steps, dtype=jnp.int32)[None, :]
    newer = jnp.where(causal, newer, NEGATIVE)
    highest = jnp.maximum(lax.optimization_barrier(jnp.max(older, axis=-1)), lax.optimization_barrier(jnp.max(newer, axis=-1)))[..., None]
    far_mass = jnp.exp(older - highest)
    near_mass = jnp.exp(newer - highest)
    total_mass = (lax.optimization_barrier(jnp.sum(far_mass, axis=-1)) + lax.optimization_barrier(jnp.sum(near_mass, axis=-1)))[..., None]
    far_weights = (far_mass / total_mass).astype(jnp.bfloat16)
    near_weights = (near_mass / total_mass).astype(jnp.bfloat16)
    blended = jnp.einsum('kgsc,cke->skge', far_weights.astype(jnp.float32), old_values.astype(jnp.float32))
    blended = blended + jnp.einsum('kgst,tke->skge', near_weights.astype(jnp.float32), new_values.astype(jnp.float32))
    return blended.reshape(steps, heads * size).astype(jnp.bfloat16)

def reference(hidden_states, context_lengths, cache_keys, cache_values, q_weight, k_weight, v_weight, o_weight, gate_weight, up_weight, down_weight, attn_gain, post_attn_gain, ffn_gain, post_ffn_gain):
    states = hidden_states.astype(jnp.float32)
    total = lax.optimization_barrier(jnp.sum(states * states, axis=1))
    normed = (states * scaling(total) * attn_gain.astype(jnp.float32)).astype(jnp.bfloat16)
    query_lin = jnp.dot(normed, q_weight, preferred_element_type=jnp.float32)
    key_lin = jnp.dot(normed, k_weight, preferred_element_type=jnp.float32)
    value_lin = jnp.dot(normed, v_weight, preferred_element_type=jnp.float32)
    positions = (context_lengths[:, None] + jnp.arange(DRAFT, dtype=jnp.int32)[None, :]).reshape(TOKENS)
    queries = rotate(query_lin.reshape(TOKENS, HEADS, HEAD_DIM), positions[:, None]).astype(jnp.bfloat16)
    new_keys = rotate(key_lin.reshape(TOKENS, KV_HEADS, HEAD_DIM), positions[:, None]).astype(jnp.bfloat16)
    draft_keys = new_keys.reshape(REQUESTS, DRAFT, KV_HEADS, HEAD_DIM)
    draft_values = value_lin.astype(jnp.bfloat16).reshape(REQUESTS, DRAFT, KV_HEADS, HEAD_DIM)
    attended = lax.map(attend_one, (queries.reshape(REQUESTS, DRAFT, HEADS, HEAD_DIM), draft_keys, draft_values, cache_keys, cache_values, context_lengths))
    attended = attended.reshape(TOKENS, HEADS * HEAD_DIM)
    mixed = jnp.dot(attended, o_weight, preferred_element_type=jnp.float32)
    total = lax.optimization_barrier(jnp.sum(mixed * mixed, axis=1))
    middle = (states + mixed * scaling(total) * post_attn_gain.astype(jnp.float32)).astype(jnp.bfloat16)
    middle_wide = middle.astype(jnp.float32)
    total = lax.optimization_barrier(jnp.sum(middle_wide * middle_wide, axis=1))
    normed_mid = (middle_wide * scaling(total) * ffn_gain.astype(jnp.float32)).astype(jnp.bfloat16)
    gate = lax.dot_general(normed_mid, gate_weight, (((1,), (1,)), ((), ())), preferred_element_type=jnp.float32)
    up = lax.dot_general(normed_mid, up_weight, (((1,), (1,)), ((), ())), preferred_element_type=jnp.float32)
    hidden = (jax.nn.gelu(gate, approximate=True) * up).astype(jnp.bfloat16)
    ffn_out = jnp.dot(hidden, down_weight, preferred_element_type=jnp.float32)
    total = lax.optimization_barrier(jnp.sum(ffn_out * ffn_out, axis=1))
    layer_output = (middle_wide + ffn_out * scaling(total) * post_ffn_gain.astype(jnp.float32)).astype(jnp.bfloat16)
    return (layer_output, draft_keys, draft_values)
```

```python
import functools

import jax
import jax.numpy as jnp
from jax import lax
from jax.experimental import pallas as pl
from jax.experimental.pallas import tpu as pltpu
from jax.sharding import PartitionSpec as P

D = 4608
HEADS = 32


EPSILON = 1e-06
NEGATIVE = -1e30


def rotate(values, positions):
    size = values.shape[-1]
    half = size // 2
    rates = 10000.0 ** (-(jnp.arange(half, dtype=jnp.float32) * 2.0) / size)
    angle = positions.astype(jnp.float32)[..., None] * rates
    cosine = jnp.cos(angle)
    sine = jnp.sin(angle)
    first = values[..., :half]
    second = values[..., half:]
    return jnp.concatenate(
        [first * cosine - second * sine, second * cosine + first * sine], axis=-1
    )


def scaling(total):
    return lax.rsqrt(total / D + EPSILON)[:, None]


def attend(queries, new_keys, new_values, cache_keys, cache_values, lengths):
    req_count, steps, heads, size = queries.shape
    shared = new_keys.shape[2]
    group = heads // shared
    scale = (D // HEADS) ** (-0.5)
    grouped = queries.reshape(req_count, steps, shared, group, size)
    older = (
        jnp.einsum("rskge,rcke->rkgsc", grouped, cache_keys, preferred_element_type=jnp.float32)
        * scale
    )
    newer = (
        jnp.einsum("rskge,rtke->rkgst", grouped, new_keys, preferred_element_type=jnp.float32)
        * scale
    )
    valid = jnp.arange(cache_keys.shape[1], dtype=jnp.int32)[None, :] < lengths[:, None]
    older = jnp.where(valid[:, None, None, None, :], older, NEGATIVE)
    causal = (
        jnp.arange(steps, dtype=jnp.int32)[:, None] >= jnp.arange(steps, dtype=jnp.int32)[None, :]
    )
    newer = jnp.where(causal, newer, NEGATIVE)
    highest = jnp.maximum(jnp.max(older, axis=-1), jnp.max(newer, axis=-1))[..., None]
    far_mass = jnp.exp(older - highest)
    near_mass = jnp.exp(newer - highest)
    total_mass = (jnp.sum(far_mass, axis=-1) + jnp.sum(near_mass, axis=-1))[..., None]
    far_weights = (far_mass / total_mass).astype(jnp.bfloat16)
    near_weights = (near_mass / total_mass).astype(jnp.bfloat16)
    blended = jnp.einsum(
        "rkgsc,rcke->rskge", far_weights, cache_values, preferred_element_type=jnp.float32
    )
    blended = blended + jnp.einsum(
        "rkgst,rtke->rskge", near_weights, new_values, preferred_element_type=jnp.float32
    )
    return blended.reshape(req_count * steps, heads * size).astype(jnp.bfloat16)


LANES = 128
BF = jnp.bfloat16
F32 = jnp.float32
DMA = pltpu.SemaphoreType.DMA


def remote(src, dst, send_sem, recv_sem, **device):
    return pltpu.make_async_remote_copy(
        src_ref=src,
        dst_ref=dst,
        send_sem=send_sem,
        recv_sem=recv_sem,
        device_id=device,
        device_id_type=pl.DeviceIdType.MESH,
    )


def greet(blks, reqs):
    b, r = lax.axis_index("blk"), lax.axis_index("req")
    barrier = pltpu.get_barrier_semaphore()
    for k in range(1, blks):
        pl.semaphore_signal(
            barrier,
            inc=1,
            device_id={"blk": lax.rem(b + k, blks)},
            device_id_type=pl.DeviceIdType.MESH,
        )
    for k in range(1, reqs):
        pl.semaphore_signal(
            barrier,
            inc=1,
            device_id={"req": lax.rem(r + k, reqs)},
            device_id_type=pl.DeviceIdType.MESH,
        )
    pl.semaphore_wait(barrier, blks + reqs - 2)
    return b, r


def diagonal(rows):
    return lax.broadcasted_iota(jnp.int32, (rows, LANES), 0) == lax.broadcasted_iota(
        jnp.int32, (rows, LANES), 1
    )


def send_sums(values, buf, send_sem, recv_sem, b, blks):
    rows = values.shape[0]
    packed = jnp.sum(jnp.where(diagonal(rows), values, 0.0), axis=0, keepdims=True)
    buf[b] = jnp.broadcast_to(packed, (8, LANES))
    for k in range(1, blks):
        remote(
            buf.at[b], buf.at[b], send_sem.at[k], recv_sem.at[k], blk=lax.rem(b + k, blks)
        ).start()


def take_sums(rows, buf, send_sem, recv_sem, b, blks):
    for k in range(1, blks):
        src = lax.rem(b + blks - k, blks)
        remote(buf.at[src], buf.at[src], send_sem.at[k], recv_sem.at[k], blk=src).wait_recv()
    total = buf[0]
    for j in range(1, blks):
        total = total + buf[j]
    for k in range(1, blks):
        src = lax.rem(b + blks - k, blks)
        remote(buf.at[b], buf.at[b], send_sem.at[k], recv_sem.at[k], blk=src).wait_send()
    spread = jnp.where(diagonal(rows), total[0:1, :], 0.0)
    return jnp.sum(spread, axis=1, keepdims=True)


def inverse(total):
    return lax.rsqrt(total / D + EPSILON)


def gather_kernel(
    blks, reqs, x_ref, gain_ref, out, scale_ref, ybuf, sums, ss, sr, s0, zsend, recv, psend, xsend
):
    b, r = greet(blks, reqs)
    per = blks // reqs
    chips = blks // 2
    x, c = b // 2, lax.rem(b, 2)
    mate = b + 1 - 2 * c
    other = lax.rem(b + 2, blks) if chips > 1 else mate
    home = b // per
    mine = lax.rem(b, per)
    states = x_ref[...].astype(F32)
    ybuf[...] = (states * gain_ref[...]).astype(BF)

    @pl.when(r != home)
    def _():
        remote(ybuf, out.at[mine, r], zsend, recv.at[mine, r], req=home).start()

    @pl.when(r == home)
    def _():
        copy = pltpu.make_async_copy(ybuf, out.at[mine, r], s0)
        copy.start()
        copy.wait()

    send_sums(jnp.sum(states * states, axis=1, keepdims=True), sums, ss, sr, b, blks)

    def visit(j, rp):
        owner = r * per + j
        slot = out.at[j, rp]

        @pl.when(jnp.logical_or(b != owner, rp != r))
        def _():
            remote(slot, slot, psend.at[j, rp], recv.at[j, rp], blk=mate).wait_recv()

        @pl.when(lax.rem(owner, 2) == c)
        def _():
            remote(slot, slot, psend.at[j, rp], recv.at[j, rp], blk=mate).start()

        @pl.when(b == owner)
        def _():
            for k in range(1, chips):
                remote(
                    slot,
                    slot,
                    xsend.at[k, rp],
                    recv.at[j, rp],
                    blk=lax.rem(b + 2 * k, blks),
                ).start()

    def finish(j, rp):
        owner = r * per + j
        slot = out.at[j, rp]

        @pl.when(lax.rem(owner, 2) == c)
        def _():
            remote(slot, slot, psend.at[j, rp], recv.at[j, rp], blk=mate).wait_send()

        @pl.when(b == owner)
        def _():
            for k in range(1, chips):
                remote(slot, slot, xsend.at[k, rp], recv.at[j, rp], blk=other).wait_send()

    for call in (visit, finish):
        for dist in range(reqs):
            for rp in (r + dist, r - dist) if dist else (r,):

                @pl.when(jnp.logical_and(rp >= 0, rp < reqs))
                def _(rp=rp):
                    for j in range(per):
                        call(j, rp)

    @pl.when(r != home)
    def _():
        remote(ybuf, out.at[mine, r], zsend, recv.at[mine, r], req=home).wait_send()

    total = take_sums(x_ref.shape[0], sums, ss, sr, b, blks)
    scale_ref[...] = jnp.broadcast_to(inverse(total), scale_ref.shape)


def chain_step(reqs, r, d, part, left, right, lsend, lrecv, rsend, rrecv):
    def step(go, first, buf, send_sem, recv_sem, nxt):
        @pl.when(go)
        def _():
            @pl.when(first)
            def _():
                remote(part.at[d], buf.at[d], send_sem.at[d], recv_sem.at[d], req=nxt).start()

            @pl.when(jnp.logical_not(first))
            def _():
                remote(part.at[d], buf.at[d], send_sem.at[d], recv_sem.at[d], req=nxt).wait_recv()
                buf[d] = (buf[d].astype(F32) + part[d].astype(F32)).astype(BF)
                remote(buf.at[d], buf.at[d], send_sem.at[d], recv_sem.at[d], req=nxt).start()

    step(r < d, r == 0, left, lsend, lrecv, r + 1)
    step(r > d, r == reqs - 1, right, rsend, rrecv, r - 1)


def chain_order(reqs):
    order = []
    for k in range(reqs):
        order.append(reqs - 1 - k // 2 if k % 2 == 0 else k // 2)
    return order


def chain_end(reqs, r, part, left, right, lsend, lrecv, rsend, rrecv, total):
    total[...] = part[r].astype(F32)

    @pl.when(r > 0)
    def _():
        remote(left.at[r], left.at[r], lsend.at[r], lrecv.at[r], req=r - 1).wait_recv()
        total[...] += left[r].astype(F32)

    @pl.when(r < reqs - 1)
    def _():
        remote(right.at[r], right.at[r], rsend.at[r], rrecv.at[r], req=r + 1).wait_recv()
        total[...] += right[r].astype(F32)

    for d in range(reqs):

        @pl.when(r < d)
        def _():
            remote(left.at[d], left.at[d], lsend.at[d], lrecv.at[d], req=r + 1).wait_send()

        @pl.when(r > d)
        def _():
            remote(right.at[d], right.at[d], rsend.at[d], rrecv.at[d], req=r - 1).wait_send()


def project_kernel(
    blks, reqs, part, scale_ref, out, left, right, lsend, lrecv, rsend, rrecv
):
    b, r = greet(blks, reqs)
    for d in chain_order(reqs):
        chain_step(reqs, r, d, part, left, right, lsend, lrecv, rsend, rrecv)
    chain_end(reqs, r, part, left, right, lsend, lrecv, rsend, rrecv, out)
    out[...] = out[...] * scale_ref[:, 0:1]


def view(ref, blk, rows=None):
    if len(ref.shape) == 2:
        width = D // lax.axis_size("blk")
        cols = pl.ds(pl.multiple_of(blk * width, LANES), width)
        if rows is None:
            return ref.at[:, cols]
        height = ref.shape[0] // lax.axis_size("req")
        return ref.at[pl.ds(pl.multiple_of(rows * height, 16), height), cols]
    return ref.at[blk] if rows is None else ref.at[blk, rows]


def middle_kernel(
    blks, reqs, part, x_ref, post_ref, gain_ref, full, mid_ref,
    rp, rx, own, sums1, sums2, psend0, precv0, xsend0, xrecv0, ss1, sr1, ss2, sr2,
    s0, zsend, recv, psend, xsend,
):
    b, r = greet(blks, reqs)
    chips = blks // 2
    x, c = b // 2, lax.rem(b, 2)
    mate = b + 1 - 2 * c
    rows = x_ref.shape[0]
    for k in list(range(1, chips)) + [0]:
        xp = lax.rem(x + k, chips)
        remote(
            view(part, 2 * xp + 1 - c), rp.at[xp], psend0.at[k], precv0.at[k], blk=mate
        ).start()
    for k in range(1, chips):
        xp = lax.rem(x + k, chips)
        remote(rp.at[xp], rp.at[xp], psend0.at[k], precv0.at[k], blk=mate).wait_recv()
        rp[xp] = (rp[xp].astype(F32) + view(part, 2 * xp + c)[...].astype(F32)).astype(BF)
        remote(rp.at[xp], rx.at[k], xsend0.at[k], xrecv0.at[k], blk=2 * xp + c).start()
    remote(rp.at[x], rp.at[x], psend0.at[0], precv0.at[0], blk=mate).wait_recv()
    mixed = view(part, b)[...].astype(F32) + rp[x].astype(F32)
    for k in range(1, chips):
        xp = lax.rem(x + k, chips)
        remote(rx.at[k], rx.at[k], xsend0.at[k], xrecv0.at[k], blk=2 * xp + c).wait_recv()
        mixed = mixed + rx[k].astype(F32)
    send_sums(jnp.sum(mixed * mixed, axis=1, keepdims=True), sums1, ss1, sr1, b, blks)
    total = take_sums(rows, sums1, ss1, sr1, b, blks)
    middle = (x_ref[...].astype(F32) + mixed * inverse(total) * post_ref[...]).astype(BF)
    mid_ref[...] = middle
    wide = middle.astype(F32)
    send_sums(jnp.sum(wide * wide, axis=1, keepdims=True), sums2, ss2, sr2, b, blks)
    total = take_sums(rows, sums2, ss2, sr2, b, blks)
    own[...] = (wide * inverse(total) * gain_ref[...]).astype(BF)
    copy = pltpu.make_async_copy(own, view(full, b, r), s0)
    copy.start()

    def spread(rp_, src, go):
        dst = view(full, b, rp_)
        if go >= 0:

            @pl.when(r + 1 < reqs)
            def _():
                remote(src, dst, zsend.at[0, rp_], recv.at[b, rp_], req=r + 1).start()

        if go <= 0:

            @pl.when(r > 0)
            def _():
                remote(src, dst, zsend.at[1, rp_], recv.at[b, rp_], req=r - 1).start()

        for k in range(1, chips):
            to = lax.rem(b + 2 * k, blks)
            remote(src, dst, xsend.at[k, rp_], recv.at[b, rp_], blk=to).start()
        remote(src, dst, psend.at[x, rp_], recv.at[b, rp_], blk=mate).start()

    def arrive(owner, rp_):
        slot = view(full, owner, rp_)
        remote(slot, slot, psend.at[0, rp_], recv.at[owner, rp_], blk=mate).wait_recv()

    def relay(rp_):
        for k in range(1, chips):
            xp = lax.rem(x + k, chips)
            owner = 2 * xp + c
            arrive(owner, rp_)
            slot = view(full, owner, rp_)
            remote(slot, slot, psend.at[xp, rp_], recv.at[owner, rp_], blk=mate).start()

    def within(rp_, call):
        @pl.when(jnp.logical_and(rp_ >= 0, rp_ < reqs))
        def _():
            call()

    spread(r, own, 0)
    for dist in range(1, reqs):

        def up():
            arrive(b, r - dist)
            spread(r - dist, view(full, b, r - dist), 1)

        def down():
            arrive(b, r + dist)
            spread(r + dist, view(full, b, r + dist), -1)

        within(r - dist, up)
        within(r + dist, down)
        if dist == 1:
            relay(r)
        else:
            within(r - dist + 1, lambda: relay(r - dist + 1))
            within(r + dist - 1, lambda: relay(r + dist - 1))
    within(r - reqs + 1, lambda: relay(r - reqs + 1))
    within(r + reqs - 1, lambda: relay(r + reqs - 1))
    copy.wait()
    for xp in range(chips):
        for d in range(reqs):
            arrive(2 * xp + 1 - c, d)
    for d in range(reqs):
        slot = view(full, b, d)

        @pl.when(jnp.logical_and(d <= r, r + 1 < reqs))
        def _():
            remote(slot, slot, zsend.at[0, d], recv.at[b, d], blk=mate).wait_send()

        @pl.when(jnp.logical_and(d >= r, r > 0))
        def _():
            remote(slot, slot, zsend.at[1, d], recv.at[b, d], blk=mate).wait_send()

        for k in range(1, chips):
            remote(slot, slot, xsend.at[k, d], recv.at[b, d], blk=mate).wait_send()
        for xp in range(chips):
            remote(slot, slot, psend.at[xp, d], recv.at[b, d], blk=mate).wait_send()
    for k in range(chips):
        remote(rp.at[0], rp.at[0], psend0.at[k], precv0.at[k], blk=mate).wait_send()
    for k in range(1, chips):
        remote(rp.at[0], rp.at[0], xsend0.at[k], xrecv0.at[k], blk=mate).wait_send()


def last_kernel(
    blks, reqs, part, mid_ref, post_ref, out,
    rp, rx, own, left, right, acc, sums, psend, precv, xsend, xrecv,
    lsend, lrecv, rsend, rrecv, ss, sr,
):
    b, r = greet(blks, reqs)
    chips = blks // 2
    x, c = b // 2, lax.rem(b, 2)
    mate = b + 1 - 2 * c
    rows = mid_ref.shape[0]
    order = chain_order(reqs)
    for d in order:
        for k in list(range(1, chips)) + [0]:
            xp = lax.rem(x + k, chips)
            remote(
                view(part, 2 * xp + 1 - c, d), rp.at[xp, d], psend.at[k, d], precv.at[k, d], blk=mate
            ).start()
    for d in order:
        for k in range(1, chips):
            xp = lax.rem(x + k, chips)
            slot = rp.at[xp, d]
            remote(slot, slot, psend.at[k, d], precv.at[k, d], blk=mate).wait_recv()
            rp[xp, d] = (rp[xp, d].astype(F32) + view(part, 2 * xp + c, d)[...].astype(F32)).astype(BF)
            remote(slot, rx.at[k, d], xsend.at[k, d], xrecv.at[k, d], blk=2 * xp + c).start()
    for d in order:
        slot = rp.at[x, d]
        remote(slot, slot, psend.at[0, d], precv.at[0, d], blk=mate).wait_recv()
        value = view(part, b, d)[...].astype(F32) + rp[x, d].astype(F32)
        for k in range(1, chips):
            slot = rx.at[k, d]
            remote(slot, slot, xsend.at[k, d], xrecv.at[k, d], blk=mate).wait_recv()
            value = value + rx[k, d].astype(F32)
        own[d] = value.astype(BF)
        chain_step(reqs, r, d, own, left, right, lsend, lrecv, rsend, rrecv)
    chain_end(reqs, r, own, left, right, lsend, lrecv, rsend, rrecv, acc)
    ffn = acc[...]
    send_sums(jnp.sum(ffn * ffn, axis=1, keepdims=True), sums, ss, sr, b, blks)
    for d in range(reqs):
        for k in range(chips):
            slot = rp.at[0, d]
            remote(slot, slot, psend.at[k, d], precv.at[k, d], blk=mate).wait_send()
            if k:
                remote(slot, slot, xsend.at[k, d], xrecv.at[k, d], blk=mate).wait_send()
    total = take_sums(rows, sums, ss, sr, b, blks)
    out[...] = (mid_ref[...].astype(F32) + ffn * inverse(total) * post_ref[...]).astype(BF)


def call(kernel, sizes, number, outs, scratch, *args):
    vmem = pl.BlockSpec(memory_space=pltpu.VMEM)
    return pl.pallas_call(
        functools.partial(kernel, *sizes),
        out_shape=outs,
        in_specs=[vmem] * len(args),
        out_specs=jax.tree.map(lambda _: vmem, outs),
        scratch_shapes=scratch,
        compiler_params=pltpu.CompilerParams(
            collective_id=number, has_side_effects=True, vmem_limit_bytes=40 * 2**20
        ),
    )(*args)


def body(
    hidden_states,
    context_lengths,
    cache_keys,
    cache_values,
    q_weight,
    k_weight,
    v_weight,
    o_weight,
    gate_weight,
    up_weight,
    down_weight,
    attn_gain,
    post_attn_gain,
    ffn_gain,
    post_ffn_gain,
):
    blks, reqs = lax.axis_size("blk"), lax.axis_size("req")
    sizes = (blks, reqs)
    per, chips = blks // reqs, blks // 2
    rows, width = hidden_states.shape
    assert blks % reqs == 0 and blks % 2 == 0 and rows <= LANES
    req_count = context_lengths.shape[0]
    steps = rows // req_count
    kv_local = cache_keys.shape[2]
    size = cache_keys.shape[3]
    query_cols = q_weight.shape[1]
    key_cols = k_weight.shape[1]
    heads_local = query_cols // size
    shape = jax.ShapeDtypeStruct
    sums = pltpu.VMEM((blks, 8, LANES), F32)
    gathered, scale = call(
        gather_kernel,
        sizes,
        0,
        (shape((per, reqs, rows, width), BF), shape((rows, LANES), F32)),
        [
            pltpu.VMEM((rows, width), BF),
            sums,
            DMA((blks,)),
            DMA((blks,)),
            DMA,
            DMA,
            DMA((per, reqs)),
            DMA((per, reqs)),
            DMA((chips, reqs)),
        ],
        hidden_states,
        attn_gain[None, :],
    )
    slices = gathered.transpose(1, 2, 0, 3).reshape(reqs * rows, per * width)
    parts = jnp.concatenate(
        [
            jnp.dot(slices, weight, preferred_element_type=F32).astype(BF)
            for weight in (q_weight, k_weight, v_weight)
        ],
        axis=1,
    )
    cols = parts.shape[1]
    joined = call(
        project_kernel,
        sizes,
        1,
        shape((rows, cols), F32),
        [pltpu.VMEM((reqs, rows, cols), BF)] * 2 + [DMA((reqs,))] * 4,
        parts.reshape(reqs, rows, cols),
        scale,
    )
    query_lin = joined[:, :query_cols]
    key_lin = joined[:, query_cols : query_cols + key_cols]
    value_lin = joined[:, query_cols + key_cols :]
    positions = (context_lengths[:, None] + jnp.arange(steps, dtype=jnp.int32)[None, :]).reshape(
        rows
    )
    queries = rotate(query_lin.reshape(rows, heads_local, size), positions[:, None]).astype(BF)
    new_keys = rotate(key_lin.reshape(rows, kv_local, size), positions[:, None]).astype(BF)
    draft_keys = new_keys.reshape(req_count, steps, kv_local, size)
    draft_values = value_lin.astype(BF).reshape(req_count, steps, kv_local, size)
    attended = attend(
        queries.reshape(req_count, steps, heads_local, size),
        draft_keys,
        draft_values,
        cache_keys,
        cache_values,
        context_lengths,
    )
    mixed = jnp.dot(attended, o_weight, preferred_element_type=F32).astype(BF)
    flat = width % LANES == 0 and rows % 16 == 0
    if not flat:
        mixed = mixed.reshape(rows, blks, width).transpose(1, 0, 2)
    full, middle = call(
        middle_kernel,
        sizes,
        2,
        (
            shape((reqs * rows, D) if flat else (blks, reqs, rows, width), BF),
            shape((rows, width), BF),
        ),
        [
            pltpu.VMEM((chips, rows, width), BF),
            pltpu.VMEM((chips, rows, width), BF),
            pltpu.VMEM((rows, width), BF),
            sums,
            sums,
        ]
        + [DMA((chips,))] * 4
        + [DMA((blks,))] * 4
        + [DMA, DMA((2, reqs)), DMA((blks, reqs)), DMA((chips, reqs)), DMA((chips, reqs))],
        mixed,
        hidden_states,
        post_attn_gain[None, :],
        ffn_gain[None, :],
    )
    if not flat:
        full = full.transpose(1, 2, 0, 3).reshape(reqs * rows, D)
    gate = lax.dot_general(full, gate_weight, (((1,), (1,)), ((), ())), preferred_element_type=F32)
    up = lax.dot_general(full, up_weight, (((1,), (1,)), ((), ())), preferred_element_type=F32)
    hidden = (jax.nn.gelu(gate, approximate=True) * up).astype(BF)
    terms = jnp.dot(hidden, down_weight, preferred_element_type=F32).astype(BF)
    if not flat:
        terms = terms.reshape(reqs, rows, blks, width).transpose(2, 0, 1, 3)
    layer_output = call(
        last_kernel,
        sizes,
        3,
        shape((rows, width), BF),
        [pltpu.VMEM((chips, reqs, rows, width), BF)] * 2
        + [pltpu.VMEM((reqs, rows, width), BF)] * 3
        + [pltpu.VMEM((rows, width), F32), sums]
        + [DMA((chips, reqs))] * 4
        + [DMA((reqs,))] * 4
        + [DMA((blks,))] * 2,
        terms,
        middle,
        post_ffn_gain[None, :],
    )
    return (layer_output, draft_keys, draft_values)


def solution(mesh):
    placed = (
        P(("groups", "req"), "blk"),
        P(("groups", "req")),
        P(("groups", "req"), None, "blk", None),
        P(("groups", "req"), None, "blk", None),
        P("req", "blk"),
        P("req", "blk"),
        P("req", "blk"),
        P("blk", None),
        P(("blk", "req"), None),
        P(("blk", "req"), None),
        P(("blk", "req"), None),
        P("blk"),
        P("blk"),
        P("blk"),
        P("blk"),
    )
    return jax.shard_map(
        body,
        mesh=mesh,
        in_specs=placed,
        out_specs=(
            P(("groups", "req"), "blk"),
            P(("groups", "req"), None, "blk", None),
            P(("groups", "req"), None, "blk", None),
        ),
        check_vma=False,
    )
```

```python
import functools
import math

import jax
import jax.numpy as jnp
from jax import lax
from jax.experimental import pallas as pl
from jax.experimental.pallas import tpu as pltpu
from jax.sharding import PartitionSpec as P

D = 4608
HEADS = 32


EPSILON = 1e-06
NEGATIVE = -1e30


def rotate(values, positions):
    size = values.shape[-1]
    half = size // 2
    rates = 10000.0 ** (-(jnp.arange(half, dtype=jnp.float32) * 2.0) / size)
    angle = positions.astype(jnp.float32)[..., None] * rates
    cosine = jnp.cos(angle)
    sine = jnp.sin(angle)
    first = values[..., :half]
    second = values[..., half:]
    return jnp.concatenate(
        [first * cosine - second * sine, second * cosine + first * sine], axis=-1
    )


def scaling(total):
    return lax.rsqrt(total / D + EPSILON)[:, None]


LANES = 128
BF = jnp.bfloat16
F32 = jnp.float32
DMA = pltpu.SemaphoreType.DMA


def remote(src, dst, send_sem, recv_sem, **device):
    return pltpu.make_async_remote_copy(
        src_ref=src,
        dst_ref=dst,
        send_sem=send_sem,
        recv_sem=recv_sem,
        device_id=device,
        device_id_type=pl.DeviceIdType.MESH,
    )


def greet(blks, reqs):
    b, r = lax.axis_index("blk"), lax.axis_index("req")
    barrier = pltpu.get_barrier_semaphore()
    for k in range(1, blks):
        pl.semaphore_signal(
            barrier,
            inc=1,
            device_id={"blk": lax.rem(b + k, blks)},
            device_id_type=pl.DeviceIdType.MESH,
        )
    for k in range(1, reqs):
        pl.semaphore_signal(
            barrier,
            inc=1,
            device_id={"req": lax.rem(r + k, reqs)},
            device_id_type=pl.DeviceIdType.MESH,
        )
    pl.semaphore_wait(barrier, blks + reqs - 2)
    return b, r


def diagonal(rows):
    return lax.broadcasted_iota(jnp.int32, (rows, LANES), 0) == lax.broadcasted_iota(
        jnp.int32, (rows, LANES), 1
    )


def send_sums(values, buf, send_sem, recv_sem, b, blks):
    rows = values.shape[0]
    packed = jnp.sum(jnp.where(diagonal(rows), values, 0.0), axis=0, keepdims=True)
    buf[b] = jnp.broadcast_to(packed, (8, LANES))
    for k in range(1, blks):
        remote(
            buf.at[b], buf.at[b], send_sem.at[k], recv_sem.at[k], blk=lax.rem(b + k, blks)
        ).start()


def take_sums(rows, buf, send_sem, recv_sem, b, blks):
    for k in range(1, blks):
        src = lax.rem(b + blks - k, blks)
        remote(buf.at[src], buf.at[src], send_sem.at[k], recv_sem.at[k], blk=src).wait_recv()
    total = buf[0]
    for j in range(1, blks):
        total = total + buf[j]
    for k in range(1, blks):
        src = lax.rem(b + blks - k, blks)
        remote(buf.at[b], buf.at[b], send_sem.at[k], recv_sem.at[k], blk=src).wait_send()
    spread = jnp.where(diagonal(rows), total[0:1, :], 0.0)
    return jnp.sum(spread, axis=1, keepdims=True)


def inverse(total):
    return lax.rsqrt(total / D + EPSILON)


def gather_kernel(
    blks, reqs, x_ref, gains, out, scale_ref, ybuf, sums, ss, sr, s0, zsend, recv, psend, xsend
):
    b, r = greet(blks, reqs)
    per = blks // reqs
    chips = blks // 2
    x, c = b // 2, lax.rem(b, 2)
    mate = b + 1 - 2 * c
    other = lax.rem(b + 2, blks) if chips > 1 else mate
    home = b // per
    mine = lax.rem(b, per)
    states = x_ref[...].astype(F32)
    ybuf[...] = (states * gains[0:1, :]).astype(BF)

    @pl.when(r != home)
    def _():
        remote(ybuf, out.at[mine, r], zsend, recv.at[mine, r], req=home).start()

    @pl.when(r == home)
    def _():
        copy = pltpu.make_async_copy(ybuf, out.at[mine, r], s0)
        copy.start()
        copy.wait()

    send_sums(jnp.sum(states * states, axis=1, keepdims=True), sums, ss, sr, b, blks)

    def visit(j, rp):
        owner = r * per + j
        slot = out.at[j, rp]

        @pl.when(jnp.logical_or(b != owner, rp != r))
        def _():
            remote(slot, slot, psend.at[j, rp], recv.at[j, rp], blk=mate).wait_recv()

        @pl.when(lax.rem(owner, 2) == c)
        def _():
            remote(slot, slot, psend.at[j, rp], recv.at[j, rp], blk=mate).start()

        @pl.when(b == owner)
        def _():
            for k in range(1, chips):
                remote(
                    slot,
                    slot,
                    xsend.at[k, rp],
                    recv.at[j, rp],
                    blk=lax.rem(b + 2 * k, blks),
                ).start()

    def finish(j, rp):
        owner = r * per + j
        slot = out.at[j, rp]

        @pl.when(lax.rem(owner, 2) == c)
        def _():
            remote(slot, slot, psend.at[j, rp], recv.at[j, rp], blk=mate).wait_send()

        @pl.when(b == owner)
        def _():
            for k in range(1, chips):
                remote(slot, slot, xsend.at[k, rp], recv.at[j, rp], blk=other).wait_send()

    for call in (visit, finish):
        for dist in range(reqs):
            for rp in (r + dist, r - dist) if dist else (r,):

                @pl.when(jnp.logical_and(rp >= 0, rp < reqs))
                def _(rp=rp):
                    for j in range(per):
                        call(j, rp)

    @pl.when(r != home)
    def _():
        remote(ybuf, out.at[mine, r], zsend, recv.at[mine, r], req=home).wait_send()

    total = take_sums(x_ref.shape[0], sums, ss, sr, b, blks)
    scale_ref[...] = jnp.broadcast_to(inverse(total), scale_ref.shape)


def chain_step(reqs, r, d, part, left, right, lsend, lrecv, rsend, rrecv):
    def step(go, first, buf, send_sem, recv_sem, nxt):
        @pl.when(go)
        def _():
            @pl.when(first)
            def _():
                remote(part.at[d], buf.at[d], send_sem.at[d], recv_sem.at[d], req=nxt).start()

            @pl.when(jnp.logical_not(first))
            def _():
                remote(part.at[d], buf.at[d], send_sem.at[d], recv_sem.at[d], req=nxt).wait_recv()
                buf[d] = (buf[d].astype(F32) + part[d].astype(F32)).astype(BF)
                remote(buf.at[d], buf.at[d], send_sem.at[d], recv_sem.at[d], req=nxt).start()

    step(r < d, r == 0, left, lsend, lrecv, r + 1)
    step(r > d, r == reqs - 1, right, rsend, rrecv, r - 1)


def chain_place(reqs, r, i):
    low = jnp.where(i < reqs - 1 - r, reqs - 1 - i, i - (reqs - 1 - r))
    high = jnp.where(i < r, i, reqs - 1 - (i - r))
    return jnp.where(i == reqs - 1, r, jnp.where(r < reqs // 2, low, high))


def chain_end(reqs, r, part, left, right, lsend, lrecv, rsend, rrecv, total):
    total[...] = part[r].astype(F32)

    @pl.when(r > 0)
    def _():
        remote(left.at[r], left.at[r], lsend.at[r], lrecv.at[r], req=r - 1).wait_recv()
        total[...] += left[r].astype(F32)

    @pl.when(r < reqs - 1)
    def _():
        remote(right.at[r], right.at[r], rsend.at[r], rrecv.at[r], req=r + 1).wait_recv()
        total[...] += right[r].astype(F32)

    for d in range(reqs):

        @pl.when(r < d)
        def _():
            remote(left.at[d], left.at[d], lsend.at[d], lrecv.at[d], req=r + 1).wait_send()

        @pl.when(r > d)
        def _():
            remote(right.at[d], right.at[d], rsend.at[d], rrecv.at[d], req=r - 1).wait_send()


def project_kernel(
    blks, reqs, part, scale_ref, out, left, right, lsend, lrecv, rsend, rrecv
):
    b, r = greet(blks, reqs)
    for i in range(reqs - 1):
        d = chain_place(reqs, r, i)
        chain_step(reqs, r, d, part, left, right, lsend, lrecv, rsend, rrecv)
    chain_end(reqs, r, part, left, right, lsend, lrecv, rsend, rrecv, out)
    out[...] = out[...] * scale_ref[:, 0:1]


def view(ref, blk, rows=None):
    if len(ref.shape) == 2:
        width = D // lax.axis_size("blk")
        cols = pl.ds(pl.multiple_of(blk * width, LANES), width)
        if rows is None:
            return ref.at[:, cols]
        height = ref.shape[0] // lax.axis_size("req")
        return ref.at[pl.ds(pl.multiple_of(rows * height, 16), height), cols]
    return ref.at[blk] if rows is None else ref.at[blk, rows]


def middle_kernel(
    blks, reqs, part, x_ref, gains, full, mid_ref, scales,
    rp, rx, own, sums1, sums2, psend0, precv0, xsend0, xrecv0, ss1, sr1, ss2, sr2,
    s0, zsend, recv, psend, xsend, csend, crecv,
):
    b, r = greet(blks, reqs)
    chips = blks // 2
    x, c = b // 2, lax.rem(b, 2)
    mate = b + 1 - 2 * c
    rows = x_ref.shape[0]
    for k in list(range(1, chips)) + [0]:
        xp = lax.rem(x + k, chips)
        remote(
            view(part, 2 * xp + 1 - c), rp.at[xp], psend0.at[k], precv0.at[k], blk=mate
        ).start()
    for k in range(1, chips):
        xp = lax.rem(x + k, chips)
        remote(rp.at[xp], rp.at[xp], psend0.at[k], precv0.at[k], blk=mate).wait_recv()
        rp[xp] = (rp[xp].astype(F32) + view(part, 2 * xp + c)[...].astype(F32)).astype(BF)
        remote(rp.at[xp], rx.at[k], xsend0.at[k], xrecv0.at[k], blk=2 * xp + c).start()
    remote(rp.at[x], rp.at[x], psend0.at[0], precv0.at[0], blk=mate).wait_recv()
    mixed = view(part, b)[...].astype(F32) + rp[x].astype(F32)
    for k in range(1, chips):
        xp = lax.rem(x + k, chips)
        remote(rx.at[k], rx.at[k], xsend0.at[k], xrecv0.at[k], blk=2 * xp + c).wait_recv()
        mixed = mixed + rx[k].astype(F32)
    send_sums(jnp.sum(mixed * mixed, axis=1, keepdims=True), sums1, ss1, sr1, b, blks)
    total = take_sums(rows, sums1, ss1, sr1, b, blks)
    middle = (x_ref[...].astype(F32) + mixed * inverse(total) * gains[1:2, :]).astype(BF)
    mid_ref[...] = middle
    wide = middle.astype(F32)
    own[...] = (wide * gains[2:3, :]).astype(BF)
    send_sums(jnp.sum(wide * wide, axis=1, keepdims=True), sums2, ss2, sr2, b, blks)
    copy = pltpu.make_async_copy(own, view(full, b, r), s0)
    copy.start()

    def spread(rp_, src, go):
        dst = view(full, b, rp_)
        if go >= 0:

            @pl.when(r + 1 < reqs)
            def _():
                remote(src, dst, zsend.at[0, rp_], recv.at[b, rp_], req=r + 1).start()

        if go <= 0:

            @pl.when(r > 0)
            def _():
                remote(src, dst, zsend.at[1, rp_], recv.at[b, rp_], req=r - 1).start()

        for k in range(1, chips):
            to = lax.rem(b + 2 * k, blks)
            remote(src, dst, xsend.at[k, rp_], recv.at[b, rp_], blk=to).start()
        remote(src, dst, psend.at[x, rp_], recv.at[b, rp_], blk=mate).start()

    def arrive(owner, rp_):
        slot = view(full, owner, rp_)
        remote(slot, slot, psend.at[0, rp_], recv.at[owner, rp_], blk=mate).wait_recv()

    def relay(rp_):
        for k in range(1, chips):
            xp = lax.rem(x + k, chips)
            owner = 2 * xp + c
            arrive(owner, rp_)
            slot = view(full, owner, rp_)
            remote(slot, slot, psend.at[xp, rp_], recv.at[owner, rp_], blk=mate).start()

    def within(rp_, call):
        @pl.when(jnp.logical_and(rp_ >= 0, rp_ < reqs))
        def _():
            call()

    spread(r, own, 0)
    total = take_sums(rows, sums2, ss2, sr2, b, blks)
    packed = jnp.sum(jnp.where(diagonal(rows), inverse(total), 0.0), axis=0, keepdims=True)
    scales[r] = jnp.broadcast_to(packed, (8, LANES))
    for k in range(1, reqs):
        to = lax.rem(r + k, reqs)
        remote(scales.at[r], scales.at[r], csend.at[k], crecv.at[k], req=to).start()
    for dist in range(1, reqs):

        def up():
            arrive(b, r - dist)
            spread(r - dist, view(full, b, r - dist), 1)

        def down():
            arrive(b, r + dist)
            spread(r + dist, view(full, b, r + dist), -1)

        within(r - dist, up)
        within(r + dist, down)
        if dist == 1:
            relay(r)
        else:
            within(r - dist + 1, lambda: relay(r - dist + 1))
            within(r + dist - 1, lambda: relay(r + dist - 1))
    within(r - reqs + 1, lambda: relay(r - reqs + 1))
    within(r + reqs - 1, lambda: relay(r + reqs - 1))
    copy.wait()
    for k in range(1, reqs):
        src = lax.rem(r + reqs - k, reqs)
        remote(scales.at[src], scales.at[src], csend.at[k], crecv.at[k], req=src).wait()
    for xp in range(chips):
        for d in range(reqs):
            arrive(2 * xp + 1 - c, d)
    for d in range(reqs):
        slot = view(full, b, d)

        @pl.when(jnp.logical_and(d <= r, r + 1 < reqs))
        def _():
            remote(slot, slot, zsend.at[0, d], recv.at[b, d], blk=mate).wait_send()

        @pl.when(jnp.logical_and(d >= r, r > 0))
        def _():
            remote(slot, slot, zsend.at[1, d], recv.at[b, d], blk=mate).wait_send()

        for k in range(1, chips):
            remote(slot, slot, xsend.at[k, d], recv.at[b, d], blk=mate).wait_send()
        for xp in range(chips):
            remote(slot, slot, psend.at[xp, d], recv.at[b, d], blk=mate).wait_send()
    for k in range(chips):
        remote(rp.at[0], rp.at[0], psend0.at[k], precv0.at[k], blk=mate).wait_send()
    for k in range(1, chips):
        remote(rp.at[0], rp.at[0], xsend0.at[k], xrecv0.at[k], blk=mate).wait_send()


def last_kernel(
    blks, reqs, part, mid_ref, gains, out,
    rp, rx, own, left, right, acc, sums, psend, precv, xsend, xrecv,
    lsend, lrecv, rsend, rrecv, ss, sr,
):
    b, r = greet(blks, reqs)
    chips = blks // 2
    x, c = b // 2, lax.rem(b, 2)
    mate = b + 1 - 2 * c
    rows = mid_ref.shape[0]
    order = [chain_place(reqs, r, i) for i in range(reqs)]
    for d in order:
        for k in list(range(1, chips)) + [0]:
            xp = lax.rem(x + k, chips)
            remote(
                view(part, 2 * xp + 1 - c, d), rp.at[xp, d], psend.at[k, d], precv.at[k, d], blk=mate
            ).start()
    for d in order:
        for k in range(1, chips):
            xp = lax.rem(x + k, chips)
            slot = rp.at[xp, d]
            remote(slot, slot, psend.at[k, d], precv.at[k, d], blk=mate).wait_recv()
            rp[xp, d] = (rp[xp, d].astype(F32) + view(part, 2 * xp + c, d)[...].astype(F32)).astype(BF)
            remote(slot, rx.at[k, d], xsend.at[k, d], xrecv.at[k, d], blk=2 * xp + c).start()
    for d in order:
        slot = rp.at[x, d]
        remote(slot, slot, psend.at[0, d], precv.at[0, d], blk=mate).wait_recv()
        value = view(part, b, d)[...].astype(F32) + rp[x, d].astype(F32)
        for k in range(1, chips):
            slot = rx.at[k, d]
            remote(slot, slot, xsend.at[k, d], xrecv.at[k, d], blk=mate).wait_recv()
            value = value + rx[k, d].astype(F32)
        own[d] = value.astype(BF)
        chain_step(reqs, r, d, own, left, right, lsend, lrecv, rsend, rrecv)
    chain_end(reqs, r, own, left, right, lsend, lrecv, rsend, rrecv, acc)
    ffn = acc[...]
    send_sums(jnp.sum(ffn * ffn, axis=1, keepdims=True), sums, ss, sr, b, blks)
    for d in range(reqs):
        for k in range(chips):
            slot = rp.at[0, d]
            remote(slot, slot, psend.at[k, d], precv.at[k, d], blk=mate).wait_send()
            if k:
                remote(slot, slot, xsend.at[k, d], xrecv.at[k, d], blk=mate).wait_send()
    total = take_sums(rows, sums, ss, sr, b, blks)
    out[...] = (mid_ref[...].astype(F32) + ffn * inverse(total) * gains[3:4, :]).astype(BF)


def attend_kernel(
    shared, group, steps, lengths, queries, new_keys, new_values, old_keys, old_values, out
):
    heads = shared * group
    rows = steps * heads
    scale = (D // HEADS) ** (-0.5)
    length = lengths[pl.program_id(0)]
    row = lax.broadcasted_iota(jnp.int32, (rows, 1), 0)
    mine, step = lax.rem(row, heads) // group, row // heads

    def scores(keys):
        value = lax.dot_general(
            queries[0], keys, (((1,), (1,)), ((), ())), preferred_element_type=F32
        )
        col = lax.broadcasted_iota(jnp.int32, (1, keys.shape[0]), 1)
        return value * scale, lax.rem(col, shared), col // shared

    older, owner, slot = scores(old_keys[0])
    owner = jnp.where(slot < length, owner, -1)
    older = jnp.where(owner == mine, older, NEGATIVE)
    newer, owner, slot = scores(new_keys[0])
    newer = jnp.where(jnp.logical_and(owner == mine, slot <= step), newer, NEGATIVE)
    highest = jnp.maximum(
        jnp.max(older, axis=1, keepdims=True), jnp.max(newer, axis=1, keepdims=True)
    )
    far, near = jnp.exp(older - highest), jnp.exp(newer - highest)
    mass = 1.0 / (jnp.sum(far, axis=1, keepdims=True) + jnp.sum(near, axis=1, keepdims=True))
    blended = jnp.dot((far * mass).astype(BF), old_values[0], preferred_element_type=F32)
    blended += jnp.dot((near * mass).astype(BF), new_values[0], preferred_element_type=F32)
    out[0] = blended.astype(BF)


def attend(queries, new_keys, new_values, cache_keys, cache_values, lengths):
    count, slots, shared, size = cache_keys.shape
    steps = queries.shape[0] // count
    group = queries.shape[1] // shared
    rows = steps * shared * group

    def block(height):
        return pl.BlockSpec((1, height, size), lambda i: (i, 0, 0))

    out = pl.pallas_call(
        functools.partial(attend_kernel, shared, group, steps),
        grid=(count,),
        out_shape=jax.ShapeDtypeStruct((count, rows, size), BF),
        in_specs=[
            pl.BlockSpec(memory_space=pltpu.SMEM),
            block(rows),
            block(steps * shared),
            block(steps * shared),
            block(slots * shared),
            block(slots * shared),
        ],
        out_specs=block(rows),
        compiler_params=pltpu.CompilerParams(vmem_limit_bytes=57 * 2**20),
    )(
        lengths,
        queries.reshape(count, rows, size),
        new_keys.reshape(count, steps * shared, size),
        new_values.reshape(count, steps * shared, size),
        cache_keys.reshape(count, slots * shared, size),
        cache_values.reshape(count, slots * shared, size),
    )
    return out.reshape(count * steps, shared * group * size)


def call(kernel, sizes, number, outs, scratch, *args):
    vmem = pl.BlockSpec(memory_space=pltpu.VMEM)
    held = 0
    for leaf in list(args) + jax.tree.leaves(outs) + scratch:
        if hasattr(leaf.dtype, "itemsize"):
            *lead, second, last = leaf.shape
            padded = math.prod(lead) * (second + 15) * (last + LANES - 1)
            held += padded * leaf.dtype.itemsize
    limit = min(held + 6 * 2**20, 60 * 2**20)
    return pl.pallas_call(
        functools.partial(kernel, *sizes),
        out_shape=outs,
        in_specs=[vmem] * len(args),
        out_specs=jax.tree.map(lambda _: vmem, outs),
        scratch_shapes=scratch,
        cost_estimate=pl.CostEstimate(flops=10**10, bytes_accessed=10**8, transcendentals=0),
        compiler_params=pltpu.CompilerParams(
            collective_id=number, has_side_effects=True, vmem_limit_bytes=limit
        ),
    )(*args)


def body(
    hidden_states,
    context_lengths,
    cache_keys,
    cache_values,
    q_weight,
    k_weight,
    v_weight,
    o_weight,
    gate_weight,
    up_weight,
    down_weight,
    attn_gain,
    post_attn_gain,
    ffn_gain,
    post_ffn_gain,
):
    blks, reqs = lax.axis_size("blk"), lax.axis_size("req")
    sizes = (blks, reqs)
    per, chips = blks // reqs, blks // 2
    rows, width = hidden_states.shape
    assert blks % reqs == 0 and blks % 2 == 0 and rows <= LANES
    req_count = context_lengths.shape[0]
    steps = rows // req_count
    kv_local = cache_keys.shape[2]
    size = cache_keys.shape[3]
    query_cols = q_weight.shape[1]
    key_cols = k_weight.shape[1]
    heads_local = query_cols // size
    shape = jax.ShapeDtypeStruct
    sums = pltpu.VMEM((blks, 8, LANES), F32)
    gains = jnp.stack([attn_gain, post_attn_gain, ffn_gain, post_ffn_gain])
    gathered, scale = call(
        gather_kernel,
        sizes,
        0,
        (shape((per, reqs, rows, width), BF), shape((rows, LANES), F32)),
        [
            pltpu.VMEM((rows, width), BF),
            sums,
            DMA((blks,)),
            DMA((blks,)),
            DMA,
            DMA,
            DMA((per, reqs)),
            DMA((per, reqs)),
            DMA((chips, reqs)),
        ],
        hidden_states,
        gains,
    )
    slices = gathered.transpose(1, 2, 0, 3).reshape(reqs * rows, per * width)
    parts = jnp.concatenate(
        [
            jnp.dot(slices, weight, preferred_element_type=F32).astype(BF)
            for weight in (q_weight, k_weight, v_weight)
        ],
        axis=1,
    )
    cols = parts.shape[1]
    joined = call(
        project_kernel,
        sizes,
        1,
        shape((rows, cols), F32),
        [pltpu.VMEM((reqs, rows, cols), BF)] * 2 + [DMA((reqs,))] * 4,
        parts.reshape(reqs, rows, cols),
        scale,
    )
    query_lin = joined[:, :query_cols]
    key_lin = joined[:, query_cols : query_cols + key_cols]
    value_lin = joined[:, query_cols + key_cols :]
    positions = (context_lengths[:, None] + jnp.arange(steps, dtype=jnp.int32)[None, :]).reshape(
        rows
    )
    queries = rotate(query_lin.reshape(rows, heads_local, size), positions[:, None]).astype(BF)
    new_keys = rotate(key_lin.reshape(rows, kv_local, size), positions[:, None]).astype(BF)
    draft_keys = new_keys.reshape(req_count, steps, kv_local, size)
    draft_values = value_lin.astype(BF).reshape(req_count, steps, kv_local, size)
    attended = attend(
        queries, draft_keys, draft_values, cache_keys, cache_values, context_lengths
    )
    mixed = jnp.dot(attended, o_weight, preferred_element_type=F32).astype(BF)
    flat = width % LANES == 0 and rows % 16 == 0
    if not flat:
        mixed = mixed.reshape(rows, blks, width).transpose(1, 0, 2)
    full, middle, scales = call(
        middle_kernel,
        sizes,
        2,
        (
            shape((reqs * rows, D) if flat else (blks, reqs, rows, width), BF),
            shape((rows, width), BF),
            shape((reqs, 8, LANES), F32),
        ),
        [
            pltpu.VMEM((chips, rows, width), BF),
            pltpu.VMEM((chips, rows, width), BF),
            pltpu.VMEM((rows, width), BF),
            sums,
            sums,
        ]
        + [DMA((chips,))] * 4
        + [DMA((blks,))] * 4
        + [DMA, DMA((2, reqs)), DMA((blks, reqs)), DMA((chips, reqs)), DMA((chips, reqs))]
        + [DMA((reqs,))] * 2,
        mixed,
        hidden_states,
        gains,
    )
    if not flat:
        full = full.transpose(1, 2, 0, 3).reshape(reqs * rows, D)
    gate = lax.dot_general(full, gate_weight, (((1,), (1,)), ((), ())), preferred_element_type=F32)
    up = lax.dot_general(full, up_weight, (((1,), (1,)), ((), ())), preferred_element_type=F32)
    scales = scales[:, 0, :rows].reshape(reqs * rows, 1)
    gate, up = gate * scales, up * scales
    hidden = (jax.nn.gelu(gate, approximate=True) * up).astype(BF)
    terms = jnp.dot(hidden, down_weight, preferred_element_type=F32).astype(BF)
    if not flat:
        terms = terms.reshape(reqs, rows, blks, width).transpose(2, 0, 1, 3)
    layer_output = call(
        last_kernel,
        sizes,
        3,
        shape((rows, width), BF),
        [pltpu.VMEM((chips, reqs, rows, width), BF)] * 2
        + [pltpu.VMEM((reqs, rows, width), BF)] * 3
        + [pltpu.VMEM((rows, width), F32), sums]
        + [DMA((chips, reqs))] * 4
        + [DMA((reqs,))] * 4
        + [DMA((blks,))] * 2,
        terms,
        middle,
        gains,
    )
    return (layer_output, draft_keys, draft_values)


def solution(mesh):
    placed = (
        P(("groups", "req"), "blk"),
        P(("groups", "req")),
        P(("groups", "req"), None, "blk", None),
        P(("groups", "req"), None, "blk", None),
        P("req", "blk"),
        P("req", "blk"),
        P("req", "blk"),
        P("blk", None),
        P(("blk", "req"), None),
        P(("blk", "req"), None),
        P(("blk", "req"), None),
        P("blk"),
        P("blk"),
        P("blk"),
        P("blk"),
    )
    return jax.shard_map(
        body,
        mesh=mesh,
        in_specs=placed,
        out_specs=(
            P(("groups", "req"), "blk"),
            P(("groups", "req"), None, "blk", None),
            P(("groups", "req"), None, "blk", None),
        ),
        check_vma=False,
    )
```

```python
import functools
import math

import jax
import jax.numpy as jnp
from jax import lax
from jax.experimental import pallas as pl
from jax.experimental.pallas import tpu as pltpu
from jax.sharding import PartitionSpec as P

D = 4608
HEADS = 32


EPSILON = 1e-06
NEGATIVE = -1e30


def rotate(values, positions):
    size = values.shape[-1]
    half = size // 2
    rates = 10000.0 ** (-(jnp.arange(half, dtype=jnp.float32) * 2.0) / size)
    angle = positions.astype(jnp.float32)[..., None] * rates
    cosine = jnp.cos(angle)
    sine = jnp.sin(angle)
    first = values[..., :half]
    second = values[..., half:]
    return jnp.concatenate(
        [first * cosine - second * sine, second * cosine + first * sine], axis=-1
    )


def scaling(total):
    return lax.rsqrt(total / D + EPSILON)[:, None]


LANES = 128
BF = jnp.bfloat16
F32 = jnp.float32
DMA = pltpu.SemaphoreType.DMA


def remote(src, dst, send_sem, recv_sem, **device):
    return pltpu.make_async_remote_copy(
        src_ref=src,
        dst_ref=dst,
        send_sem=send_sem,
        recv_sem=recv_sem,
        device_id=device,
        device_id_type=pl.DeviceIdType.MESH,
    )


def greet(blks, reqs):
    b, r = lax.axis_index("blk"), lax.axis_index("req")
    barrier = pltpu.get_barrier_semaphore()
    for k in range(1, blks):
        pl.semaphore_signal(
            barrier,
            inc=1,
            device_id={"blk": lax.rem(b + k, blks)},
            device_id_type=pl.DeviceIdType.MESH,
        )
    for k in range(1, reqs):
        pl.semaphore_signal(
            barrier,
            inc=1,
            device_id={"req": lax.rem(r + k, reqs)},
            device_id_type=pl.DeviceIdType.MESH,
        )
    pl.semaphore_wait(barrier, blks + reqs - 2)
    return b, r


def diagonal(rows):
    return lax.broadcasted_iota(jnp.int32, (rows, LANES), 0) == lax.broadcasted_iota(
        jnp.int32, (rows, LANES), 1
    )


def send_sums(values, buf, send_sem, recv_sem, b, blks):
    rows = values.shape[0]
    packed = jnp.sum(jnp.where(diagonal(rows), values, 0.0), axis=0, keepdims=True)
    buf[b] = jnp.broadcast_to(packed, (8, LANES))
    for k in range(1, blks):
        remote(
            buf.at[b], buf.at[b], send_sem.at[k], recv_sem.at[k], blk=lax.rem(b + k, blks)
        ).start()


def take_sums(rows, buf, send_sem, recv_sem, b, blks):
    for k in range(1, blks):
        src = lax.rem(b + blks - k, blks)
        remote(buf.at[src], buf.at[src], send_sem.at[k], recv_sem.at[k], blk=src).wait_recv()
    total = buf[0]
    for j in range(1, blks):
        total = total + buf[j]
    for k in range(1, blks):
        src = lax.rem(b + blks - k, blks)
        remote(buf.at[b], buf.at[b], send_sem.at[k], recv_sem.at[k], blk=src).wait_send()
    spread = jnp.where(diagonal(rows), total[0:1, :], 0.0)
    return jnp.sum(spread, axis=1, keepdims=True)


def inverse(total):
    return lax.rsqrt(total / D + EPSILON)


def gather_kernel(
    blks, reqs, x_ref, gain_ref, out, scale_ref, ybuf, sums, ss, sr, s0, zsend, recv, psend, xsend
):
    b, r = greet(blks, reqs)
    per = blks // reqs
    chips = blks // 2
    x, c = b // 2, lax.rem(b, 2)
    mate = b + 1 - 2 * c
    other = lax.rem(b + 2, blks) if chips > 1 else mate
    home = b // per
    mine = lax.rem(b, per)
    states = x_ref[...].astype(F32)
    ybuf[...] = (states * gain_ref[...][None, :]).astype(BF)

    @pl.when(r != home)
    def _():
        remote(ybuf, out.at[mine, r], zsend, recv.at[mine, r], req=home).start()

    @pl.when(r == home)
    def _():
        copy = pltpu.make_async_copy(ybuf, out.at[mine, r], s0)
        copy.start()
        copy.wait()

    send_sums(jnp.sum(states * states, axis=1, keepdims=True), sums, ss, sr, b, blks)

    def visit(j, rp):
        owner = r * per + j
        slot = out.at[j, rp]

        @pl.when(jnp.logical_or(b != owner, rp != r))
        def _():
            remote(slot, slot, psend.at[j, rp], recv.at[j, rp], blk=mate).wait_recv()

        @pl.when(lax.rem(owner, 2) == c)
        def _():
            remote(slot, slot, psend.at[j, rp], recv.at[j, rp], blk=mate).start()

        @pl.when(b == owner)
        def _():
            for k in range(1, chips):
                remote(
                    slot,
                    slot,
                    xsend.at[k, rp],
                    recv.at[j, rp],
                    blk=lax.rem(b + 2 * k, blks),
                ).start()

    def finish(j, rp):
        owner = r * per + j
        slot = out.at[j, rp]

        @pl.when(lax.rem(owner, 2) == c)
        def _():
            remote(slot, slot, psend.at[j, rp], recv.at[j, rp], blk=mate).wait_send()

        @pl.when(b == owner)
        def _():
            for k in range(1, chips):
                remote(slot, slot, xsend.at[k, rp], recv.at[j, rp], blk=other).wait_send()

    for call in (visit, finish):
        for dist in range(reqs):
            for rp in (r + dist, r - dist) if dist else (r,):

                @pl.when(jnp.logical_and(rp >= 0, rp < reqs))
                def _(rp=rp):
                    for j in range(per):
                        call(j, rp)

    @pl.when(r != home)
    def _():
        remote(ybuf, out.at[mine, r], zsend, recv.at[mine, r], req=home).wait_send()

    total = take_sums(x_ref.shape[0], sums, ss, sr, b, blks)
    scale_ref[...] = jnp.broadcast_to(inverse(total), scale_ref.shape)


def chain_step(reqs, r, d, part, left, right, lsend, lrecv, rsend, rrecv):
    def step(go, first, buf, send_sem, recv_sem, nxt):
        @pl.when(go)
        def _():
            @pl.when(first)
            def _():
                remote(part.at[d], buf.at[d], send_sem.at[d], recv_sem.at[d], req=nxt).start()

            @pl.when(jnp.logical_not(first))
            def _():
                remote(part.at[d], buf.at[d], send_sem.at[d], recv_sem.at[d], req=nxt).wait_recv()
                buf[d] = (buf[d].astype(F32) + part[d].astype(F32)).astype(BF)
                remote(buf.at[d], buf.at[d], send_sem.at[d], recv_sem.at[d], req=nxt).start()

    step(r < d, r == 0, left, lsend, lrecv, r + 1)
    step(r > d, r == reqs - 1, right, rsend, rrecv, r - 1)


def chain_place(reqs, r, i):
    low = jnp.where(i < reqs - 1 - r, reqs - 1 - i, i - (reqs - 1 - r))
    high = jnp.where(i < r, i, reqs - 1 - (i - r))
    return jnp.where(i == reqs - 1, r, jnp.where(r < reqs // 2, low, high))


def chain_end(reqs, r, part, left, right, lsend, lrecv, rsend, rrecv, total):
    total[...] = part[r].astype(F32)

    @pl.when(r > 0)
    def _():
        remote(left.at[r], left.at[r], lsend.at[r], lrecv.at[r], req=r - 1).wait_recv()
        total[...] += left[r].astype(F32)

    @pl.when(r < reqs - 1)
    def _():
        remote(right.at[r], right.at[r], rsend.at[r], rrecv.at[r], req=r + 1).wait_recv()
        total[...] += right[r].astype(F32)

    for d in range(reqs):

        @pl.when(r < d)
        def _():
            remote(left.at[d], left.at[d], lsend.at[d], lrecv.at[d], req=r + 1).wait_send()

        @pl.when(r > d)
        def _():
            remote(right.at[d], right.at[d], rsend.at[d], rrecv.at[d], req=r - 1).wait_send()


def project_kernel(
    blks, reqs, part, scale_ref, out, left, right, lsend, lrecv, rsend, rrecv
):
    b, r = greet(blks, reqs)
    for i in range(reqs - 1):
        d = chain_place(reqs, r, i)
        chain_step(reqs, r, d, part, left, right, lsend, lrecv, rsend, rrecv)
    chain_end(reqs, r, part, left, right, lsend, lrecv, rsend, rrecv, out)
    out[...] = out[...] * scale_ref[:, 0:1]


def view(ref, blk, rows=None):
    if len(ref.shape) == 2:
        width = D // lax.axis_size("blk")
        cols = pl.ds(pl.multiple_of(blk * width, LANES), width)
        if rows is None:
            return ref.at[:, cols]
        height = ref.shape[0] // lax.axis_size("req")
        return ref.at[pl.ds(pl.multiple_of(rows * height, 16), height), cols]
    return ref.at[blk] if rows is None else ref.at[blk, rows]


def middle_kernel(
    blks, reqs, part, x_ref, post_ref, gain_ref, full, mid_ref, scales,
    rp, rx, own, sums1, sums2, psend0, precv0, xsend0, xrecv0, ss1, sr1, ss2, sr2,
    s0, zsend, recv, psend, xsend, csend, crecv,
):
    b, r = greet(blks, reqs)
    chips = blks // 2
    x, c = b // 2, lax.rem(b, 2)
    mate = b + 1 - 2 * c
    rows = x_ref.shape[0]
    for k in list(range(1, chips)) + [0]:
        xp = lax.rem(x + k, chips)
        remote(
            view(part, 2 * xp + 1 - c), rp.at[xp], psend0.at[k], precv0.at[k], blk=mate
        ).start()
    for k in range(1, chips):
        xp = lax.rem(x + k, chips)
        remote(rp.at[xp], rp.at[xp], psend0.at[k], precv0.at[k], blk=mate).wait_recv()
        rp[xp] = (rp[xp].astype(F32) + view(part, 2 * xp + c)[...].astype(F32)).astype(BF)
        remote(rp.at[xp], rx.at[k], xsend0.at[k], xrecv0.at[k], blk=2 * xp + c).start()
    remote(rp.at[x], rp.at[x], psend0.at[0], precv0.at[0], blk=mate).wait_recv()
    mixed = view(part, b)[...].astype(F32) + rp[x].astype(F32)
    for k in range(1, chips):
        xp = lax.rem(x + k, chips)
        remote(rx.at[k], rx.at[k], xsend0.at[k], xrecv0.at[k], blk=2 * xp + c).wait_recv()
        mixed = mixed + rx[k].astype(F32)
    send_sums(jnp.sum(mixed * mixed, axis=1, keepdims=True), sums1, ss1, sr1, b, blks)
    total = take_sums(rows, sums1, ss1, sr1, b, blks)
    middle = (x_ref[...].astype(F32) + mixed * inverse(total) * post_ref[...][None, :]).astype(BF)
    mid_ref[...] = middle
    wide = middle.astype(F32)
    own[...] = (wide * gain_ref[...][None, :]).astype(BF)
    send_sums(jnp.sum(wide * wide, axis=1, keepdims=True), sums2, ss2, sr2, b, blks)
    copy = pltpu.make_async_copy(own, view(full, b, r), s0)
    copy.start()

    def spread(rp_, src, go):
        dst = view(full, b, rp_)
        if go >= 0:

            @pl.when(r + 1 < reqs)
            def _():
                remote(src, dst, zsend.at[0, rp_], recv.at[b, rp_], req=r + 1).start()

        if go <= 0:

            @pl.when(r > 0)
            def _():
                remote(src, dst, zsend.at[1, rp_], recv.at[b, rp_], req=r - 1).start()

        for k in range(1, chips):
            to = lax.rem(b + 2 * k, blks)
            remote(src, dst, xsend.at[k, rp_], recv.at[b, rp_], blk=to).start()
        remote(src, dst, psend.at[x, rp_], recv.at[b, rp_], blk=mate).start()

    def arrive(owner, rp_):
        slot = view(full, owner, rp_)
        remote(slot, slot, psend.at[0, rp_], recv.at[owner, rp_], blk=mate).wait_recv()

    def relay(rp_):
        for k in range(1, chips):
            xp = lax.rem(x + k, chips)
            owner = 2 * xp + c
            arrive(owner, rp_)
            slot = view(full, owner, rp_)
            remote(slot, slot, psend.at[xp, rp_], recv.at[owner, rp_], blk=mate).start()

    def within(rp_, call):
        @pl.when(jnp.logical_and(rp_ >= 0, rp_ < reqs))
        def _():
            call()

    spread(r, own, 0)
    total = take_sums(rows, sums2, ss2, sr2, b, blks)
    packed = jnp.sum(jnp.where(diagonal(rows), inverse(total), 0.0), axis=0, keepdims=True)
    scales[r] = jnp.broadcast_to(packed, (8, LANES))
    for k in range(1, reqs):
        to = lax.rem(r + k, reqs)
        remote(scales.at[r], scales.at[r], csend.at[k], crecv.at[k], req=to).start()
    for dist in range(1, reqs):

        def up():
            arrive(b, r - dist)
            spread(r - dist, view(full, b, r - dist), 1)

        def down():
            arrive(b, r + dist)
            spread(r + dist, view(full, b, r + dist), -1)

        within(r - dist, up)
        within(r + dist, down)
        if dist == 1:
            relay(r)
        else:
            within(r - dist + 1, lambda: relay(r - dist + 1))
            within(r + dist - 1, lambda: relay(r + dist - 1))
    within(r - reqs + 1, lambda: relay(r - reqs + 1))
    within(r + reqs - 1, lambda: relay(r + reqs - 1))
    copy.wait()
    for k in range(1, reqs):
        src = lax.rem(r + reqs - k, reqs)
        remote(scales.at[src], scales.at[src], csend.at[k], crecv.at[k], req=src).wait()
    for xp in range(chips):
        for d in range(reqs):
            arrive(2 * xp + 1 - c, d)
    for d in range(reqs):
        slot = view(full, b, d)

        @pl.when(jnp.logical_and(d <= r, r + 1 < reqs))
        def _():
            remote(slot, slot, zsend.at[0, d], recv.at[b, d], blk=mate).wait_send()

        @pl.when(jnp.logical_and(d >= r, r > 0))
        def _():
            remote(slot, slot, zsend.at[1, d], recv.at[b, d], blk=mate).wait_send()

        for k in range(1, chips):
            remote(slot, slot, xsend.at[k, d], recv.at[b, d], blk=mate).wait_send()
        for xp in range(chips):
            remote(slot, slot, psend.at[xp, d], recv.at[b, d], blk=mate).wait_send()
    for k in range(chips):
        remote(rp.at[0], rp.at[0], psend0.at[k], precv0.at[k], blk=mate).wait_send()
    for k in range(1, chips):
        remote(rp.at[0], rp.at[0], xsend0.at[k], xrecv0.at[k], blk=mate).wait_send()


def last_kernel(
    blks, reqs, part, mid_ref, post_ref, out,
    rp, rx, own, left, right, acc, sums, psend, precv, xsend, xrecv,
    lsend, lrecv, rsend, rrecv, ss, sr,
):
    b, r = greet(blks, reqs)
    chips = blks // 2
    x, c = b // 2, lax.rem(b, 2)
    mate = b + 1 - 2 * c
    rows = mid_ref.shape[0]
    order = [chain_place(reqs, r, i) for i in range(reqs)]
    for d in order:
        for k in list(range(1, chips)) + [0]:
            xp = lax.rem(x + k, chips)
            remote(
                view(part, 2 * xp + 1 - c, d), rp.at[xp, d], psend.at[k, d], precv.at[k, d], blk=mate
            ).start()
    for d in order:
        for k in range(1, chips):
            xp = lax.rem(x + k, chips)
            slot = rp.at[xp, d]
            remote(slot, slot, psend.at[k, d], precv.at[k, d], blk=mate).wait_recv()
            rp[xp, d] = (rp[xp, d].astype(F32) + view(part, 2 * xp + c, d)[...].astype(F32)).astype(BF)
            remote(slot, rx.at[k, d], xsend.at[k, d], xrecv.at[k, d], blk=2 * xp + c).start()
    for d in order:
        slot = rp.at[x, d]
        remote(slot, slot, psend.at[0, d], precv.at[0, d], blk=mate).wait_recv()
        value = view(part, b, d)[...].astype(F32) + rp[x, d].astype(F32)
        for k in range(1, chips):
            slot = rx.at[k, d]
            remote(slot, slot, xsend.at[k, d], xrecv.at[k, d], blk=mate).wait_recv()
            value = value + rx[k, d].astype(F32)
        own[d] = value.astype(BF)
        chain_step(reqs, r, d, own, left, right, lsend, lrecv, rsend, rrecv)
    chain_end(reqs, r, own, left, right, lsend, lrecv, rsend, rrecv, acc)
    ffn = acc[...]
    send_sums(jnp.sum(ffn * ffn, axis=1, keepdims=True), sums, ss, sr, b, blks)
    for d in range(reqs):
        for k in range(chips):
            slot = rp.at[0, d]
            remote(slot, slot, psend.at[k, d], precv.at[k, d], blk=mate).wait_send()
            if k:
                remote(slot, slot, xsend.at[k, d], xrecv.at[k, d], blk=mate).wait_send()
    total = take_sums(rows, sums, ss, sr, b, blks)
    out[...] = (mid_ref[...].astype(F32) + ffn * inverse(total) * post_ref[...][None, :]).astype(BF)


def attend(queries, new_keys, new_values, cache_keys, cache_values, lengths):
    req_count, steps, heads, size = queries.shape
    shared = new_keys.shape[2]
    group = heads // shared
    scale = (D // HEADS) ** (-0.5)
    grouped = queries.reshape(req_count, steps, shared, group, size)
    older = (
        jnp.einsum("rskge,rcke->rkgsc", grouped, cache_keys, preferred_element_type=jnp.float32)
        * scale
    )
    newer = (
        jnp.einsum("rskge,rtke->rkgst", grouped, new_keys, preferred_element_type=jnp.float32)
        * scale
    )
    valid = jnp.arange(cache_keys.shape[1], dtype=jnp.int32)[None, :] < lengths[:, None]
    older = jnp.where(valid[:, None, None, None, :], older, NEGATIVE)
    causal = (
        jnp.arange(steps, dtype=jnp.int32)[:, None] >= jnp.arange(steps, dtype=jnp.int32)[None, :]
    )
    newer = jnp.where(causal, newer, NEGATIVE)
    highest = jnp.maximum(jnp.max(older, axis=-1), jnp.max(newer, axis=-1))[..., None]
    far_mass = jnp.exp(older - highest)
    near_mass = jnp.exp(newer - highest)
    total_mass = (jnp.sum(far_mass, axis=-1) + jnp.sum(near_mass, axis=-1))[..., None]
    far_weights = (far_mass / total_mass).astype(jnp.bfloat16)
    near_weights = (near_mass / total_mass).astype(jnp.bfloat16)
    blended = jnp.einsum(
        "rkgsc,rcke->rskge", far_weights, cache_values, preferred_element_type=jnp.float32
    )
    blended = blended + jnp.einsum(
        "rkgst,rtke->rskge", near_weights, new_values, preferred_element_type=jnp.float32
    )
    return blended.reshape(req_count * steps, heads * size).astype(jnp.bfloat16)


def call(kernel, sizes, number, outs, scratch, *args):
    vmem = pl.BlockSpec(memory_space=pltpu.VMEM)
    held = 0
    for leaf in list(args) + jax.tree.leaves(outs) + scratch:
        if hasattr(leaf.dtype, "itemsize"):
            *lead, second, last = (1,) + leaf.shape
            padded = math.prod(lead) * (second + 15) * (last + LANES - 1)
            held += padded * leaf.dtype.itemsize
    limit = min(held + 6 * 2**20, 60 * 2**20)
    return pl.pallas_call(
        functools.partial(kernel, *sizes),
        out_shape=outs,
        in_specs=[vmem] * len(args),
        out_specs=jax.tree.map(lambda _: vmem, outs),
        scratch_shapes=scratch,
        cost_estimate=pl.CostEstimate(flops=10**10, bytes_accessed=10**8, transcendentals=0),
        compiler_params=pltpu.CompilerParams(
            collective_id=number, has_side_effects=True, vmem_limit_bytes=limit
        ),
    )(*args)


def body(
    hidden_states,
    context_lengths,
    cache_keys,
    cache_values,
    q_weight,
    k_weight,
    v_weight,
    o_weight,
    gate_weight,
    up_weight,
    down_weight,
    attn_gain,
    post_attn_gain,
    ffn_gain,
    post_ffn_gain,
):
    blks, reqs = lax.axis_size("blk"), lax.axis_size("req")
    sizes = (blks, reqs)
    per, chips = blks // reqs, blks // 2
    rows, width = hidden_states.shape
    assert blks % reqs == 0 and blks % 2 == 0 and rows <= LANES
    req_count = context_lengths.shape[0]
    steps = rows // req_count
    kv_local = cache_keys.shape[2]
    size = cache_keys.shape[3]
    query_cols = q_weight.shape[1]
    key_cols = k_weight.shape[1]
    heads_local = query_cols // size
    shape = jax.ShapeDtypeStruct
    sums = pltpu.VMEM((blks, 8, LANES), F32)
    gathered, scale = call(
        gather_kernel,
        sizes,
        0,
        (shape((per, reqs, rows, width), BF), shape((rows, LANES), F32)),
        [
            pltpu.VMEM((rows, width), BF),
            sums,
            DMA((blks,)),
            DMA((blks,)),
            DMA,
            DMA,
            DMA((per, reqs)),
            DMA((per, reqs)),
            DMA((chips, reqs)),
        ],
        hidden_states,
        attn_gain,
    )
    slices = gathered.transpose(1, 2, 0, 3).reshape(reqs * rows, per * width)
    parts = jnp.concatenate(
        [
            jnp.dot(slices, weight, preferred_element_type=F32).astype(BF)
            for weight in (q_weight, k_weight, v_weight)
        ],
        axis=1,
    )
    cols = parts.shape[1]
    joined = call(
        project_kernel,
        sizes,
        1,
        shape((rows, cols), F32),
        [pltpu.VMEM((reqs, rows, cols), BF)] * 2 + [DMA((reqs,))] * 4,
        parts.reshape(reqs, rows, cols),
        scale,
    )
    query_lin = joined[:, :query_cols]
    key_lin = joined[:, query_cols : query_cols + key_cols]
    value_lin = joined[:, query_cols + key_cols :]
    positions = (context_lengths[:, None] + jnp.arange(steps, dtype=jnp.int32)[None, :]).reshape(
        rows
    )
    queries = rotate(query_lin.reshape(rows, heads_local, size), positions[:, None]).astype(BF)
    new_keys = rotate(key_lin.reshape(rows, kv_local, size), positions[:, None]).astype(BF)
    draft_keys = new_keys.reshape(req_count, steps, kv_local, size)
    draft_values = value_lin.astype(BF).reshape(req_count, steps, kv_local, size)
    attended = attend(
        queries.reshape(req_count, steps, heads_local, size), draft_keys, draft_values, cache_keys, cache_values, context_lengths
    )
    mixed = jnp.dot(attended, o_weight, preferred_element_type=F32).astype(BF)
    flat = width % LANES == 0 and rows % 16 == 0
    if not flat:
        mixed = mixed.reshape(rows, blks, width).transpose(1, 0, 2)
    full, middle, scales = call(
        middle_kernel,
        sizes,
        2,
        (
            shape((reqs * rows, D) if flat else (blks, reqs, rows, width), BF),
            shape((rows, width), BF),
            shape((reqs, 8, LANES), F32),
        ),
        [
            pltpu.VMEM((chips, rows, width), BF),
            pltpu.VMEM((chips, rows, width), BF),
            pltpu.VMEM((rows, width), BF),
            sums,
            sums,
        ]
        + [DMA((chips,))] * 4
        + [DMA((blks,))] * 4
        + [DMA, DMA((2, reqs)), DMA((blks, reqs)), DMA((chips, reqs)), DMA((chips, reqs))]
        + [DMA((reqs,))] * 2,
        mixed,
        hidden_states,
        post_attn_gain,
        ffn_gain,
    )
    if not flat:
        full = full.transpose(1, 2, 0, 3).reshape(reqs * rows, D)
    gate = lax.dot_general(full, gate_weight, (((1,), (1,)), ((), ())), preferred_element_type=F32)
    up = lax.dot_general(full, up_weight, (((1,), (1,)), ((), ())), preferred_element_type=F32)
    scales = scales[:, 0, :rows].reshape(reqs * rows, 1)
    gate, up = gate * scales, up * scales
    hidden = (jax.nn.gelu(gate, approximate=True) * up).astype(BF)
    terms = jnp.dot(hidden, down_weight, preferred_element_type=F32).astype(BF)
    if not flat:
        terms = terms.reshape(reqs, rows, blks, width).transpose(2, 0, 1, 3)
    layer_output = call(
        last_kernel,
        sizes,
        3,
        shape((rows, width), BF),
        [pltpu.VMEM((chips, reqs, rows, width), BF)] * 2
        + [pltpu.VMEM((reqs, rows, width), BF)] * 3
        + [pltpu.VMEM((rows, width), F32), sums]
        + [DMA((chips, reqs))] * 4
        + [DMA((reqs,))] * 4
        + [DMA((blks,))] * 2,
        terms,
        middle,
        post_ffn_gain,
    )
    return (layer_output, draft_keys, draft_values)


def solution(mesh):
    placed = (
        P(("groups", "req"), "blk"),
        P(("groups", "req")),
        P(("groups", "req"), None, "blk", None),
        P(("groups", "req"), None, "blk", None),
        P("req", "blk"),
        P("req", "blk"),
        P("req", "blk"),
        P("blk", None),
        P(("blk", "req"), None),
        P(("blk", "req"), None),
        P(("blk", "req"), None),
        P("blk"),
        P("blk"),
        P("blk"),
        P("blk"),
    )
    return jax.shard_map(
        body,
        mesh=mesh,
        in_specs=placed,
        out_specs=(
            P(("groups", "req"), "blk"),
            P(("groups", "req"), None, "blk", None),
            P(("groups", "req"), None, "blk", None),
        ),
        check_vma=False,
    )
```
